32 devices in a mesh: rep: 8 (over z, core), shard: 4 (over y, x).
Axes of the slice: x: 2, y: 2, z: 4, core: 2. Of those that a mesh axis runs over, the one named last changes fastest.
Arguments:
- hidden_in: bfloat16 [16384, 1536], P(('rep', 'shard')), may hold values from -6 to 6
- seg_ids: int32 [16384], P(('rep', 'shard')), may hold values from -1 to 1, as said below
- norm_gain: float32 [1536], replicated, may hold values from 0.1 to 1.9
- in_weight: bfloat16 [1536, 6448], P('shard'), may hold values from -0.15625 to 0.15625
- conv_weight: float32 [4, 3328], replicated, may hold values from -3 to 3
- conv_bias: float32 [3328], replicated, may hold values from -3 to 3
- dt_bias: float32 [48], replicated, may hold values from -6.5 to -3
- a_log: float32 [48], replicated, may hold values from 0 to 2.77
- skip_gain: float32 [48], replicated, may hold values from 0.5 to 2
- gate_gain: float32 [3072], replicated, may hold values from 0.1 to 1.9
- out_weight: bfloat16 [3072, 1536], P('shard'), may hold values from -0.109375 to 0.109375
- cotangent: bfloat16 [16384, 1536], P(('rep', 'shard')), may hold values from -6 to 6
Outputs:
- block_out: bfloat16 [16384, 1536], P(('rep', 'shard'))
- input_grad: float32 [16384, 1536], P(('rep', 'shard'))
- norm_gain_grad: float32 [1536], replicated
- in_weight_grad: float32 [1536, 6448], P('shard')
- conv_weight_grad: float32 [4, 3328], replicated
- conv_bias_grad: float32 [3328], replicated
- dt_bias_grad: float32 [48], replicated
- a_log_grad: float32 [48], replicated
- skip_gain_grad: float32 [48], replicated
- gate_gain_grad: float32 [3072], replicated
- out_weight_grad: float32 [3072, 1536], P('shard')
The draws below stay inside these ranges and needn't reach their ends.
Inputs may be any that keep to these rules, and one draw needn't show every extreme that they name: `seg_ids`: within one device's 512 rows each id other than -1 marks one whole sequence of consecutive rows that begins at a multiple of 256; ids of sequences rise along the rows; no sequence spans two devices; some sequence has exactly 512 rows.
All inputs are finite; a program needn't handle non-finite values.
Results may differ from the reference program's by a relative error of at most 0.015.
Values may be sent and summed in bfloat16 or wider, within the bound.
No kernel may reach another device: no remote copies, remote signals or barrier semaphores. Data moves between devices by JAX's collectives and lax.ppermute only.
A program may use at most 256 MiB of HBM per device.

```python
from functools import partial
import jax
import jax.numpy as jnp
from jax import lax

D = 1536
INNER = 3072
HEADS = 48
CONV = 4
STRETCH = 256
TILES_DEV = 2
TOK_DEV = 512
TOKENS = 16384
XBC = 3328
F_IN = 6448


def one_device(key, device_id):
    lengths = jax.random.randint(key, (TILES_DEV,), max(1, STRETCH // 4), TOK_DEV + 1).astype(jnp.int32)
    lengths = jnp.where(device_id == 0, TOK_DEV, lengths)
    lengths = jnp.where(device_id == 1, STRETCH, lengths)
    lengths = jnp.where(device_id == 2, STRETCH - 1, lengths)
    position = jnp.arange(TOK_DEV, dtype=jnp.int32)
    seg_rows = jnp.full((TOK_DEV,), -1, jnp.int32)
    next_tile = jnp.int32(0)
    for number in range(TILES_DEV):
        tiles_needed = (lengths[number] + STRETCH - 1) // STRETCH
        placed = next_tile + tiles_needed <= TILES_DEV
        first_row = next_tile * STRETCH
        inside = placed & (position >= first_row) & (position < first_row + lengths[number])
        seg_rows = jnp.where(inside, number, seg_rows)
        next_tile = jnp.where(placed, next_tile + tiles_needed, next_tile)
    return seg_rows.astype(jnp.int32)


def draw_seg_ids(key, part):
    device_count = TOKENS // TOK_DEV
    key_list = jax.random.split(key, device_count)
    device_ids = jnp.arange(device_count, dtype=jnp.int32)
    return jax.vmap(one_device)(key_list, device_ids).reshape(-1)


def shard_levels(own_key, extent, cuts, smallest, high):
    gain = 1.0
    for dim, parts in cuts:
        steps = jax.random.uniform(jax.random.fold_in(jax.random.fold_in(own_key, 6), dim), (parts,), jnp.float32, smallest / len(cuts), high / len(cuts))
        gain = gain * jnp.repeat(jnp.exp(steps), extent[dim] // parts).reshape((-1,) + (1,) * (len(extent) - 1 - dim))
    return gain


def scatter_about(stream_key, extent, scale, reach, cuts=(), kind=jnp.bfloat16):
    loudness = shard_levels(stream_key, extent, cuts, -0.22, 0.18) if cuts else 1.0
    values = jax.random.normal(stream_key, extent, jnp.float32) * scale * loudness
    return jnp.minimum(jnp.maximum(values, -reach), reach).astype(kind)


def setup_inputs(seed: int = 0) -> dict:
    seeds = jax.random.split(jax.random.key(seed), 13)
    return {
        "hidden_in": scatter_about(seeds[0], (TOKENS, D), 1.0, 6.0, ((0, 32),)),
        "seg_ids": draw_seg_ids(jax.random.fold_in(seeds[12], 71), 0),
        "norm_gain": jnp.clip(1.0 + 0.18 * jax.random.normal(seeds[2], (D,), jnp.float32), 0.1, 1.9),
        "in_weight": scatter_about(seeds[3], (D, F_IN), D ** -0.5, 0.15625, ((0, 4),)),
        "conv_weight": scatter_about(seeds[4], (CONV, XBC), CONV ** -0.5, 3.0, (), jnp.float32),
        "conv_bias": scatter_about(seeds[5], (XBC,), 0.5, 3.0, (), jnp.float32),
        "dt_bias": jnp.clip(jax.random.uniform(seeds[6], (HEADS,), jnp.float32, -6.5, -3.0), -6.5, -3.0),
        "a_log": jnp.clip(jax.random.uniform(seeds[7], (HEADS,), jnp.float32, 0.0, 2.77), 0.0, 2.77),
        "skip_gain": jnp.clip(jax.random.uniform(seeds[8], (HEADS,), jnp.float32, 0.5, 2.0), 0.5, 2.0),
        "gate_gain": jnp.clip(1.0 + 0.18 * jax.random.normal(seeds[9], (INNER,), jnp.float32), 0.1, 1.9),
        "out_weight": scatter_about(seeds[10], (INNER, D), INNER ** -0.5, 0.109375, ((0, 4),)),
        "cotangent": scatter_about(seeds[11], (TOKENS, D), 1.0, 6.0, ((0, 32),)),
    }


epsilon = 1e-05
HIGHEST = lax.Precision.HIGHEST

@jax.custom_vjp
def low(v):
    return lax.optimization_barrier(v.astype(jnp.bfloat16)).astype(jnp.float32)

@jax.custom_vjp
def low_back(v):
    return v

def low_keep(v):
    return (low(v), None)

def low_pass(kept, grad):
    return (grad,)

def back_keep(v):
    return (v, None)

def back_low(kept, grad):
    return (low(grad),)
low.defvjp(low_keep, low_pass)
low_back.defvjp(back_keep, back_low)

def rms_in(hidden, norm_gain):
    return hidden * lax.rsqrt(lax.optimization_barrier(jnp.mean(hidden * hidden, axis=-1, keepdims=True)) + epsilon) * norm_gain

def scan_block(head_count, carry_state, pieces):
    signal, writer, reader, step_size, log_decay, starts = pieces
    block_len = signal.shape[0]
    running = jnp.cumsum(log_decay, axis=0)
    local_index = jnp.cumsum(starts).astype(jnp.int32)
    carried = (local_index == 0).astype(jnp.float32)
    position = lax.broadcasted_iota(jnp.int32, (block_len, block_len), 0)
    column = lax.broadcasted_iota(jnp.int32, (block_len, block_len), 1)
    allowed = (local_index[:, None] == local_index[None, :]) & (column <= position)
    spread = running.T[:, :, None] - running.T[:, None, :]
    decays = jnp.exp(jnp.where(allowed[None], spread, -jnp.inf))
    scores = jnp.dot(reader, writer.T, precision=HIGHEST)
    mixing = decays * scores[None] * step_size.T[:, None, :]
    per_head = signal.reshape(block_len, head_count, -1)
    intra_out = jnp.einsum('hij,jhp->ihp', mixing, per_head, precision=HIGHEST)
    inter_out = jnp.einsum('in,hnp->ihp', reader, carry_state, precision=HIGHEST) * (jnp.exp(running) * carried[:, None])[:, :, None]
    reach_end = (local_index == local_index[-1]).astype(jnp.float32)
    end_weight = jnp.exp(running[-1][None, :] - running) * reach_end[:, None] * step_size
    next_state = carry_state * (jnp.exp(running[-1]) * carried[-1])[:, None, None] + jnp.einsum('jn,jh,jhp->hnp', writer, end_weight, per_head, precision=HIGHEST)
    return (next_state, (intra_out + inter_out).reshape(block_len, -1))

def mixer(projected, seg_ids, conv_weight, conv_bias, dt_bias, a_log, skip_gain, gate_gain, block_len):
    inner_dim = gate_gain.shape[0]
    head_count = dt_bias.shape[0]
    conv_width = conv_bias.shape[0]
    state_dim = (conv_width - inner_dim) // 2
    tap_count = conv_weight.shape[0]
    row_count = projected.shape[0]
    head_dim = inner_dim // head_count
    gate_cols = projected[:, :inner_dim]
    conv_in = projected[:, inner_dim:inner_dim + conv_width]
    dt_raw = projected[:, inner_dim + conv_width:]
    starts = jnp.concatenate([jnp.ones((1,), jnp.int32), (seg_ids[1:] != seg_ids[:-1]).astype(jnp.int32)])
    seq_index = jnp.cumsum(starts).astype(jnp.int32)
    summed = conv_bias + conv_weight[tap_count - 1] * conv_in
    for offset in range(1, tap_count):
        shifted = jnp.concatenate([jnp.zeros((offset, conv_width), jnp.float32), conv_in[:-offset]])
        earlier = jnp.concatenate([jnp.full((offset,), -1, jnp.int32), seq_index[:-offset]])
        usable = (earlier == seq_index).astype(jnp.float32)
        summed = summed + conv_weight[tap_count - 1 - offset] * shifted * usable[:, None]
    conv_out = jax.nn.silu(summed)
    signal = conv_out[:, :inner_dim]
    writer = conv_out[:, inner_dim:inner_dim + state_dim]
    reader = conv_out[:, inner_dim + state_dim:]
    step_size = jax.nn.softplus(dt_raw + dt_bias)
    log_decay = -jnp.exp(a_log) * step_size
    block_count = row_count // block_len

    def blocks(value):
        return value.reshape((block_count, block_len) + value.shape[1:])
    initial = jnp.zeros((head_count, state_dim, head_dim), jnp.float32)
    final_state, scanned = lax.scan(jax.checkpoint(partial(scan_block, head_count)), initial, (blocks(signal), blocks(writer), blocks(reader), blocks(step_size), blocks(log_decay), blocks(starts)))
    ssm_out = scanned.reshape(row_count, inner_dim) + (signal.reshape(row_count, head_count, head_dim) * skip_gain[:, None]).reshape(row_count, inner_dim)
    gated = ssm_out * jax.nn.silu(gate_cols)
    live = (seg_ids >= 0).astype(jnp.float32)
    return gated * lax.rsqrt(lax.optimization_barrier(jnp.mean(gated * gated, axis=-1, keepdims=True)) + epsilon) * gate_gain * live[:, None]

def layer(hidden, seg_ids, norm_gain, in_w, conv_weight, conv_bias, dt_bias, a_log, skip_gain, gate_gain, out_w):
    normed = low(rms_in(hidden, norm_gain))
    projected = low_back(low(jnp.dot(normed, in_w, precision=HIGHEST)))
    mixer_out = low(mixer(projected, seg_ids, conv_weight, conv_bias, dt_bias, a_log, skip_gain, gate_gain, STRETCH))
    return hidden + jnp.dot(mixer_out, out_w, precision=HIGHEST)

def reference(hidden_in, seg_ids, norm_gain, in_weight, conv_weight, conv_bias, dt_bias, a_log, skip_gain, gate_gain, out_weight, cotangent):
    groups = TOKENS // TOK_DEV
    hidden = hidden_in.astype(jnp.float32).reshape(groups, TOK_DEV, D)
    seg_rows = seg_ids.reshape(groups, TOK_DEV)
    cot_rows = cotangent.astype(jnp.float32).reshape(groups, TOK_DEV, D)
    params = (norm_gain, in_weight.astype(jnp.float32), conv_weight, conv_bias, dt_bias, a_log, skip_gain, gate_gain, out_weight.astype(jnp.float32))

    def visit(totals, pieces):
        hid_rows, seg_part, cot_part = pieces

        def forward(hid, g_norm, in_w, c_w, c_b, b_dt, l_a, s_g, g_g, out_w):
            return layer(hid, seg_part, g_norm, in_w, c_w, c_b, b_dt, l_a, s_g, g_g, out_w)
        result, back = jax.vjp(forward, hid_rows, *params)
        grads = back(cot_part)
        totals = tuple((acc_grad + new_grad for acc_grad, new_grad in zip(totals, grads[1:])))
        return (totals, (result.astype(jnp.bfloat16), grads[0]))
    initial = tuple((jnp.zeros_like(param) for param in params))
    totals, (outputs, input_rows) = lax.scan(visit, initial, (hidden, seg_rows, cot_rows))
    return (outputs.reshape(TOKENS, D), input_rows.reshape(TOKENS, D), totals[0], totals[1], totals[2], totals[3], totals[4], totals[5], totals[6], totals[7], totals[8])
```

```python
from functools import partial

import jax
import jax.numpy as jnp
from jax import lax
from jax.experimental import pallas as pl
from jax.experimental.pallas import tpu as pltpu
from jax.sharding import Mesh, PartitionSpec as P

EPS = 1e-05
HIGHEST = lax.Precision.HIGHEST
F32 = jnp.float32
BF16 = jnp.bfloat16
LC = 128
HEADS_STEP = 8
HD = 64


def dot(a, b, dims=((1,), (0,)), precision=None):
    return lax.dot_general(
        a, b, (dims, ((), ())), preferred_element_type=F32, precision=precision
    )


NT = ((1,), (1,))


def sigmoid(v):
    return 0.5 * jnp.tanh(0.5 * v) + 0.5


def silu_and_slope(pre):
    s = sigmoid(pre)
    value = pre * s
    return value, s + value * (1.0 - s)


def split3(value, head_count):
    lane = lax.broadcasted_iota(jnp.int32, value.shape, 1)
    value = jnp.where(lane < head_count, value, 0.0)
    hi = value.astype(BF16)
    rest = value - hi.astype(F32)
    mid = rest.astype(BF16)
    low = (rest - mid.astype(F32)).astype(BF16)
    first = (hi.astype(F32) + pltpu.roll(mid.astype(F32), head_count, 1)).astype(BF16)
    return jnp.concatenate([first, low], axis=1)


def conv_forward(padded, row, lanes, weight, bias, taps, masks, rows):
    window = padded[pl.ds(row, rows + 8), lanes]
    pre = bias + weight[taps - 1 : taps, :] * window[8 : 8 + rows, :]
    for offset in range(1, taps):
        pre = pre + weight[taps - 1 - offset : taps - offset, :] * (
            window[8 - offset : 8 - offset + rows, :] * masks[offset - 1, pl.ds(row, rows), :]
        )
    return pre


def forward_kernel(
    head_count,
    x_in, bc_in, dt_in, wx, bx, wbc, bbc, dt_bias, a_log, skip, u_ref, allowed, edges, ex, exa,
    x_out, slope_out, y_out, s0_out, bc_out, bcs_out, stack_out, heads_out, at_out,
    padded, cb, bt, xdt, xw, state, d1, ea, ew, ax,
):
    rows = x_in.shape[0]
    chunks = rows // LC
    width = x_in.shape[1]
    taps = wx.shape[0]
    group = pl.program_id(0)

    @pl.when(group == 0)
    def _():
        padded[0:8, :] = jnp.zeros((8, width), F32)
        padded[8:, 0:256] = bc_in[...].astype(F32)
        tri = (
            lax.broadcasted_iota(jnp.int32, (LC, LC), 0)
            >= lax.broadcasted_iota(jnp.int32, (LC, LC), 1)
        ).astype(F32)
        for c in range(chunks):
            row = c * LC
            here = slice(row, row + LC)
            for t in range(2):
                lanes = slice(t * 128, t * 128 + 128)
                pre = conv_forward(
                    padded, row, lanes, wbc[:, lanes], bbc[:, lanes], taps, u_ref, LC
                )
                value, slope = silu_and_slope(pre)
                bc_out[here, lanes] = value.astype(BF16)
                bcs_out[here, lanes] = slope
            writer = bc_out[here, 0:128]
            reader = bc_out[here, 128:256]
            cb[here, :] = dot(reader, writer, NT) * allowed[here, :]
            bt[:, here] = writer.astype(F32).T.astype(BF16)
            v = dt_in[here, :].astype(F32) + dt_bias[...]
            step = jnp.maximum(v, 0.0) + jnp.log1p(jnp.exp(-jnp.abs(v)))
            decay = -jnp.exp(a_log[...]) * step
            a = dot(tri, decay, precision=HIGHEST)
            last = a[LC - 1 : LC, :]
            heads_out[0, here, :] = step
            heads_out[1, here, :] = decay
            at_out[c] = a.T
            stack_out[0, here, :] = split3(step, head_count)
            stack_out[1, here, :] = split3(jnp.exp(a) * edges[0, here, :], head_count)
            stack_out[2, here, :] = split3(jnp.exp(last - a) * edges[1, here, :], head_count)
            stack_out[3, here, :] = split3(a, head_count)

    padded[8:, :] = x_in[...].astype(F32)
    state[...] = jnp.zeros_like(state)

    def chunk(c, carry):
        row = pl.multiple_of(c * LC, LC)
        here = pl.ds(row, LC)
        d1[...] = dot(stack_out[0, here, :], ex[...])
        ea[...] = dot(stack_out[1, here, :], ex[...])
        ew[...] = dot(stack_out[2, here, :], ex[...])
        ax[...] = dot(stack_out[3, here, :], exa[...])
        s0 = state[...].astype(BF16)
        s0_out[pl.ds(c, 1), :, :] = s0[None]
        low = lax.broadcasted_iota(jnp.int32, (LC, 128), 1) < HD
        for p in range(width // 128):
            lanes = slice(p * 128, p * 128 + 128)
            pre = conv_forward(padded, row, lanes, wx[:, lanes], bx[:, lanes], taps, u_ref, LC)
            value, slope = silu_and_slope(pre)
            x_out[here, lanes] = value.astype(BF16)
            slope_out[here, lanes] = slope.astype(BF16)
            scaled = value * d1[:, lanes]
            xdt[:, lanes] = scaled.astype(BF16)
            xw[:, lanes] = (scaled * ew[:, lanes]).astype(BF16)
        reader = bc_out[here, 128:256]
        inter = dot(reader, s0)
        scores = cb[here, :]
        ats = at_out[c, pl.ds(pl.multiple_of(group * HEADS_STEP, 8), HEADS_STEP), :]
        for p in range(width // 128):
            lanes = slice(p * 128, p * 128 + 128)
            mixes = []
            for k in range(2):
                head = 2 * p + k
                arow = ats[head : head + 1, :]
                acol = ax[:, head * 128 : head * 128 + 128]
                mixes.append((jnp.exp(jnp.minimum(acol - arow, 0.0)) * scores).astype(BF16))
            pair = xdt[:, lanes]
            zero = jnp.zeros_like(pair)
            both = jnp.concatenate([jnp.where(low, pair, zero), jnp.where(low, zero, pair)], axis=0)
            y = dot(jnp.concatenate(mixes, axis=1), both)
            y = y + ea[:, lanes] * inter[:, lanes]
            y = y + skip[:, lanes] * x_out[here, lanes].astype(F32)
            y_out[here, lanes] = y.astype(BF16)
        state[...] = state[...] * ea[LC - 1 : LC, :] + dot(bt[:, here], xw[...])
        return carry

    lax.fori_loop(0, chunks, chunk, 0)


def run_forward(proj, inner, head_count, state_dim, conv_w, conv_b, dt_bias, a_log, skip, masks):
    rows = proj.shape[0]
    chunks = rows // LC
    width = HEADS_STEP * HD
    groups = inner // width
    taps = conv_w.shape[0]
    bc = 2 * state_dim
    const = lambda *index: (lambda g: index)
    full = lambda shape: pl.BlockSpec(shape, lambda g: (0,) * len(shape))
    col = lambda lead: pl.BlockSpec((lead, width), lambda g: (0, g))
    out_shape = (
        jax.ShapeDtypeStruct((rows, inner), BF16),
        jax.ShapeDtypeStruct((rows, inner), BF16),
        jax.ShapeDtypeStruct((rows, inner), BF16),
        jax.ShapeDtypeStruct((chunks, state_dim, inner), BF16),
        jax.ShapeDtypeStruct((rows, bc), BF16),
        jax.ShapeDtypeStruct((rows, bc), F32),
        jax.ShapeDtypeStruct((4, rows, 256), BF16),
        jax.ShapeDtypeStruct((2, rows, 128), F32),
        jax.ShapeDtypeStruct((chunks, 128, LC), F32),
    )
    return pl.pallas_call(
        partial(forward_kernel, head_count),
        grid=(groups,),
        in_specs=[
            col(rows),
            pl.BlockSpec((rows, bc), const(0, inner // bc)),
            pl.BlockSpec((rows, 128), const(0, (inner + bc) // 128)),
            col(taps),
            col(1),
            pl.BlockSpec((taps, bc), const(0, inner // bc)),
            pl.BlockSpec((1, bc), const(0, inner // bc)),
            full((1, 128)),
            full((1, 128)),
            col(1),
            full((taps - 1, rows, 128)),
            full((rows, 128)),
            full((2, rows, 128)),
            col(256),
            pl.BlockSpec((256, HEADS_STEP * 128), lambda g: (0, g)),
        ],
        out_specs=[
            col(rows),
            col(rows),
            col(rows),
            pl.BlockSpec((chunks, state_dim, width), lambda g: (0, 0, g)),
            full((rows, bc)),
            full((rows, bc)),
            full((4, rows, 256)),
            full((2, rows, 128)),
            full((chunks, 128, LC)),
        ],
        out_shape=out_shape,
        scratch_shapes=[
            pltpu.VMEM((rows + 8, width), F32),
            pltpu.VMEM((rows, 128), F32),
            pltpu.VMEM((state_dim, rows), BF16),
            pltpu.VMEM((LC, width), BF16),
            pltpu.VMEM((LC, width), BF16),
            pltpu.VMEM((state_dim, width), F32),
            pltpu.VMEM((LC, width), F32),
            pltpu.VMEM((LC, width), F32),
            pltpu.VMEM((LC, width), F32),
            pltpu.VMEM((LC, HEADS_STEP * 128), F32),
        ],
        cost_estimate=pl.CostEstimate(
            flops=20_000_000_000, bytes_accessed=20_000_000, transcendentals=0
        ),
        name="scan_forward",
    )(
        proj, proj, proj, conv_w, conv_b, conv_w, conv_b, dt_bias, a_log, skip,
        masks["u"], masks["allowed"], masks["edges"], masks["ex"], masks["exa"],
    )


def norm_kernel(y_ref, z_ref, dm_ref, gain, live_ref, mixer_out, d_y, d_z, gg_out, gated_s, slope_s):
    rows = y_ref.shape[0]
    inner = y_ref.shape[1]
    tiles = inner // 128
    live = live_ref[...]
    square = jnp.zeros((rows, 128), F32)
    mixed = jnp.zeros((rows, 128), F32)
    for t in range(tiles):
        lanes = slice(t * 128, t * 128 + 128)
        z = z_ref[:, lanes].astype(F32)
        gated = y_ref[:, lanes].astype(F32) * (z * sigmoid(z))
        gated_s[:, lanes] = gated
        square = square + gated * gated
        mixed = mixed + gated * (gain[:, lanes] * (dm_ref[:, lanes].astype(F32) * live))
    q = lax.rsqrt(jnp.sum(square, axis=1, keepdims=True) * (1.0 / inner) + EPS)
    r = jnp.sum(mixed, axis=1, keepdims=True) * (1.0 / inner)
    q = jnp.broadcast_to(q, (rows, 128))
    back = q * q * q * r
    keep = q * live

    @pl.when(pl.program_id(0) == 0)
    def _():
        gg_out[...] = jnp.zeros_like(gg_out)

    for t in range(tiles):
        lanes = slice(t * 128, t * 128 + 128)
        z = z_ref[:, lanes].astype(F32)
        s = sigmoid(z)
        gate = z * s
        slope = s + gate * (1.0 - s)
        gated = gated_s[:, lanes]
        scale = gain[:, lanes]
        mixer_out[:, lanes] = (gated * keep * scale).astype(BF16)
        m = dm_ref[:, lanes].astype(F32) * keep
        gg_out[:, lanes] += jnp.sum((m * gated).reshape(rows // 8, 8, 128), axis=0)
        d_gated = m * scale - gated * back
        d_y[:, lanes] = (d_gated * gate).astype(BF16)
        d_z[:, lanes] = (d_gated * y_ref[:, lanes].astype(F32) * slope).astype(BF16)


def run_norm(y, z, d_mixer, gain, live):
    rows, inner = y.shape
    block = 128
    spec = pl.BlockSpec((block, inner), lambda i: (i, 0))
    return pl.pallas_call(
        norm_kernel,
        grid=(rows // block,),
        in_specs=[
            spec, spec, spec,
            pl.BlockSpec((1, inner), lambda i: (0, 0)),
            pl.BlockSpec((block, 128), lambda i: (i, 0)),
        ],
        out_specs=[spec, spec, spec, pl.BlockSpec((8, inner), lambda i: (0, 0))],
        out_shape=(
            jax.ShapeDtypeStruct((rows, inner), BF16),
            jax.ShapeDtypeStruct((rows, inner), BF16),
            jax.ShapeDtypeStruct((rows, inner), BF16),
            jax.ShapeDtypeStruct((8, inner), F32),
        ),
        scratch_shapes=[pltpu.VMEM((block, inner), F32), pltpu.VMEM((block, 128), F32)],
        cost_estimate=pl.CostEstimate(
            flops=10_000_000_000, bytes_accessed=20_000_000, transcendentals=0
        ),
        name="gated_norm",
    )(y, z, d_mixer, gain, live)


def conv_backward(padded, row, lanes, x_ref, weight, taps, masks):
    x = x_ref[pl.ds(row, LC), lanes].astype(F32)
    window = padded[pl.ds(row, LC + 8), lanes]
    d0 = window[0:LC, :]
    fold = lambda v: jnp.sum(v.reshape(LC // 8, 8, 128), axis=0)
    result = weight[taps - 1 : taps, :] * d0
    sums = [fold(d0), fold(d0 * x)]
    for offset in range(1, taps):
        moved = window[offset : offset + LC, :] * masks[offset - 1, pl.ds(row, LC), :]
        result = result + weight[taps - 1 - offset : taps - offset, :] * moved
        sums.append(fold(moved * x))
    return result, sums


def backward_kernel(
    head_count,
    dy_ref, x_ref, slope_ref, x_in, bc_in, s0_ref, bc_ref, bcs_ref, stack, heads, at_ref, dt_in,
    wx, wbc, dt_bias, a_log, skip, um_ref, allowed_t, ex, exa, hs,
    dx_out, sums_out, dbc_out, sums_bc_out, ddt_out, small_out,
    padded, grad, cbt, dcbt, ct, d_writer, d_reader, prow, qcol, hsum, sgrow,
    d1, ea, ew, ax, inter, gb, dye, xdt, xw, sacc,
):
    rows = x_ref.shape[0]
    chunks = rows // LC
    width = x_ref.shape[1]
    taps = wx.shape[0]
    group = pl.program_id(0)
    tiles = width // 128

    @pl.when(group == 0)
    def _():
        padded[rows:, :] = jnp.zeros((8, width), F32)
        for c in range(chunks):
            here = slice(c * LC, c * LC + LC)
            writer = bc_ref[here, 0:128]
            reader = bc_ref[here, 128:256]
            cbt[here, :] = dot(writer, reader, NT) * allowed_t[here, :]
            ct[:, here] = reader.astype(F32).T.astype(BF16)
        for ref in (dcbt, d_writer, d_reader, prow, qcol, hsum, sgrow):
            ref[...] = jnp.zeros_like(ref)

    grad[...] = jnp.zeros_like(grad)
    low = lax.broadcasted_iota(jnp.int32, (LC, 128), 1) < HD
    lane = lax.broadcasted_iota(jnp.int32, (LC, 128), 1)

    def chunk(i, carry):
        c = chunks - 1 - i
        row = pl.multiple_of(c * LC, LC)
        here = pl.ds(row, LC)
        d1[...] = dot(stack[0, here, :], ex[...])
        ea[...] = dot(stack[1, here, :], ex[...])
        ew[...] = dot(stack[2, here, :], ex[...])
        ax[...] = dot(stack[3, here, :], exa[...])
        writer = bc_ref[here, 0:128]
        reader = bc_ref[here, 128:256]
        s0 = s0_ref[c]
        g = grad[...]
        g_low = g.astype(BF16)
        inter[...] = dot(reader, s0)
        gb[...] = dot(writer, g_low) * ew[...]
        fold = jnp.sum((s0.astype(F32) * g).reshape(s0.shape[0] // 8, 8, width), axis=0)
        fold = fold * ea[LC - 1 : LC, :]
        sgrow[pl.ds(pl.multiple_of(c * 8, 8), 8), :] += dot(fold.astype(BF16), hs[...])
        for p in range(tiles):
            lanes = slice(p * 128, p * 128 + 128)
            x = x_ref[here, lanes].astype(F32)
            dy = dy_ref[here, lanes].astype(F32)
            scaled = x * d1[:, lanes]
            xdt[:, lanes] = scaled.astype(BF16)
            xw[:, lanes] = (scaled * ew[:, lanes]).astype(BF16)
            weighted = dy * ea[:, lanes]
            dye[:, lanes] = weighted.astype(BF16)
            sacc[1, :, lanes] = (x * gb[:, lanes]).astype(BF16)
            sacc[2, :, lanes] = (weighted * inter[:, lanes]).astype(BF16)
            sacc[3, :, lanes] = (dy * x).astype(BF16)
        d_reader[here, :] += dot(dye[...], s0, NT)
        d_writer[here, :] += dot(xw[...], g_low, NT)
        scores = cbt[here, :]
        group_rows = pl.ds(pl.multiple_of(group * HEADS_STEP, 8), HEADS_STEP)
        ats = at_ref[c, group_rows, :]
        for p in range(tiles):
            lanes = slice(p * 128, p * 128 + 128)
            pair = dy_ref[here, lanes]
            src = xdt[:, lanes]
            zero = jnp.zeros_like(pair)
            src2 = jnp.concatenate([jnp.where(low, src, zero), jnp.where(low, zero, src)], axis=0)
            pair2 = jnp.concatenate([jnp.where(low, pair, zero), jnp.where(low, zero, pair)], axis=0)
            dm = dot(src2, pair, NT)
            mixes = []
            for k in range(2):
                head = 2 * p + k
                index = group * HEADS_STEP + head
                arow = ats[head : head + 1, :]
                acol = ax[:, head * 128 : head * 128 + 128]
                e = jnp.exp(jnp.minimum(arow - acol, 0.0))
                mixes.append((e * scores).astype(BF16))
                t = e * dm[k * LC : k * LC + LC, :]
                dcbt[here, :] += t
                qq = t * scores
                prow.at[c, group_rows, :][head : head + 1, :] = jnp.sum(qq, axis=0, keepdims=True)
                qcol[here, :] = jnp.where(
                    lane == index, jnp.sum(qq, axis=1, keepdims=True), qcol[here, :]
                )
            x = x_ref[here, lanes].astype(F32)
            dxdt = dot(jnp.concatenate(mixes, axis=1), pair2) + gb[:, lanes]
            sacc[0, :, lanes] = (x * dxdt).astype(BF16)
            dx = d1[:, lanes] * dxdt + skip[:, lanes] * pair.astype(F32)
            padded[here, lanes] = dx * slope_ref[here, lanes].astype(F32)
        for k in range(4):
            hsum[k, here, :] += dot(sacc[k], hs[...])
        grad[...] = g * ea[LC - 1 : LC, :] + dot(ct[:, here], dye[...])
        return carry

    lax.fori_loop(0, chunks, chunk, 0)

    sums_out[...] = jnp.zeros_like(sums_out)

    def conv_chunk(c, carry):
        row = pl.multiple_of(c * LC, LC)
        for p in range(tiles):
            lanes = slice(p * 128, p * 128 + 128)
            result, sums = conv_backward(padded, row, lanes, x_in, wx[:, lanes], taps, um_ref)
            dx_out[pl.ds(row, LC), lanes] = result.astype(BF16)
            for k in range(taps + 1):
                sums_out[k, :, lanes] += sums[k]
        return carry

    lax.fori_loop(0, chunks, conv_chunk, 0)

    @pl.when(group == pl.num_programs(0) - 1)
    def _():
        total_a = jnp.zeros((8, 128), F32)
        total_dt = jnp.zeros((8, 128), F32)
        total_skip = jnp.zeros((8, 128), F32)
        upper = (
            lax.broadcasted_iota(jnp.int32, (LC, LC), 0)
            <= lax.broadcasted_iota(jnp.int32, (LC, LC), 1)
        ).astype(F32)
        at_end = lax.broadcasted_iota(jnp.int32, (LC, 128), 0) == LC - 1
        fold = lambda v: jnp.sum(v.reshape(LC // 8, 8, 128), axis=0)
        sums_bc_out[...] = jnp.zeros_like(sums_bc_out)
        for c in range(chunks):
            here = slice(c * LC, c * LC + LC)
            writer = bc_ref[here, 0:128]
            reader = bc_ref[here, 128:256]
            d_scores = dcbt[here, :] * allowed_t[here, :]
            d_w = d_writer[here, :] + dot(d_scores.astype(BF16), reader)
            d_r = d_reader[here, :] + dot(d_scores.T.astype(BF16), writer)
            padded[here, 0:128] = d_w * bcs_ref[here, 0:128]
            padded[here, 128:256] = d_r * bcs_ref[here, 128:256]
            step = heads[0, here, :]
            decay = heads[1, here, :]
            q_state = step * hsum[1, here, :]
            da = prow[c].T - qcol[here, :] + hsum[2, here, :] - q_state
            ends = jnp.sum(q_state, axis=0, keepdims=True) + jnp.sum(
                sgrow[c * 8 : c * 8 + 8, :], axis=0, keepdims=True
            )
            da = da + jnp.where(at_end, ends, 0.0)
            d_decay = dot(upper, da, precision=HIGHEST)
            d_step = hsum[0, here, :] - jnp.exp(a_log[...]) * d_decay
            d_raw = d_step * sigmoid(dt_in[here, :].astype(F32) + dt_bias[...])
            d_raw = jnp.where(lane < head_count, d_raw, 0.0)
            ddt_out[here, :] = d_raw.astype(BF16)
            total_dt = total_dt + fold(d_raw)
            total_a = total_a + fold(d_decay * decay)
            total_skip = total_skip + fold(hsum[3, here, :])
        small_out[0] = total_dt
        small_out[1] = total_a
        small_out[2] = total_skip
        for c in range(chunks):
            row = c * LC
            for p in range(2):
                lanes = slice(p * 128, p * 128 + 128)
                result, sums = conv_backward(padded, row, lanes, bc_in, wbc[:, lanes], taps, um_ref)
                dbc_out[row : row + LC, lanes] = result.astype(BF16)
                for k in range(taps + 1):
                    sums_bc_out[k, :, lanes] += sums[k]


def run_backward(dy, saved, proj, head_count, state_dim, conv_w, dt_bias, a_log, skip, masks):
    x, slope, _, s0, bc_val, bc_slope, stack, heads, at = saved
    rows, inner = dy.shape
    chunks = rows // LC
    width = HEADS_STEP * HD
    groups = inner // width
    taps = conv_w.shape[0]
    bc = 2 * state_dim
    const = lambda *index: (lambda g: index)
    full = lambda shape: pl.BlockSpec(shape, lambda g: (0,) * len(shape))
    col = lambda lead: pl.BlockSpec((lead, width), lambda g: (0, g))
    return pl.pallas_call(
        partial(backward_kernel, head_count),
        grid=(groups,),
        in_specs=[
            col(rows),
            col(rows),
            col(rows),
            col(rows),
            pl.BlockSpec((rows, bc), const(0, inner // bc)),
            pl.BlockSpec((chunks, state_dim, width), lambda g: (0, 0, g)),
            full((rows, bc)),
            full((rows, bc)),
            full((4, rows, 256)),
            full((2, rows, 128)),
            full((chunks, 128, LC)),
            pl.BlockSpec((rows, 128), const(0, (inner + bc) // 128)),
            col(taps),
            pl.BlockSpec((taps, bc), const(0, inner // bc)),
            full((1, 128)),
            full((1, 128)),
            col(1),
            full((taps - 1, rows, 128)),
            full((rows, 128)),
            col(256),
            pl.BlockSpec((256, HEADS_STEP * 128), lambda g: (0, g)),
            pl.BlockSpec((width, 128), lambda g: (g, 0)),
        ],
        out_specs=[
            col(rows),
            pl.BlockSpec((taps + 1, 8, width), lambda g: (0, 0, g)),
            full((rows, bc)),
            full((taps + 1, 8, bc)),
            full((rows, 128)),
            full((3, 8, 128)),
        ],
        out_shape=(
            jax.ShapeDtypeStruct((rows, inner), BF16),
            jax.ShapeDtypeStruct((taps + 1, 8, inner), F32),
            jax.ShapeDtypeStruct((rows, bc), BF16),
            jax.ShapeDtypeStruct((taps + 1, 8, bc), F32),
            jax.ShapeDtypeStruct((rows, 128), BF16),
            jax.ShapeDtypeStruct((3, 8, 128), F32),
        ),
        scratch_shapes=[
            pltpu.VMEM((rows + 8, width), F32),
            pltpu.VMEM((state_dim, width), F32),
            pltpu.VMEM((rows, 128), F32),
            pltpu.VMEM((rows, 128), F32),
            pltpu.VMEM((state_dim, rows), BF16),
            pltpu.VMEM((rows, 128), F32),
            pltpu.VMEM((rows, 128), F32),
            pltpu.VMEM((chunks, 128, LC), F32),
            pltpu.VMEM((rows, 128), F32),
            pltpu.VMEM((4, rows, 128), F32),
            pltpu.VMEM((chunks * 8, 128), F32),
            pltpu.VMEM((LC, width), F32),
            pltpu.VMEM((LC, width), F32),
            pltpu.VMEM((LC, width), F32),
            pltpu.VMEM((LC, HEADS_STEP * 128), F32),
            pltpu.VMEM((LC, width), F32),
            pltpu.VMEM((LC, width), F32),
            pltpu.VMEM((LC, width), BF16),
            pltpu.VMEM((LC, width), BF16),
            pltpu.VMEM((LC, width), BF16),
            pltpu.VMEM((4, LC, width), BF16),
        ],
        cost_estimate=pl.CostEstimate(
            flops=40_000_000_000, bytes_accessed=20_000_000, transcendentals=0
        ),
        name="scan_backward",
    )(
        dy, x, slope, proj, proj, s0, bc_val, bc_slope, stack, heads, at, proj,
        conv_w, conv_w, dt_bias, a_log, skip, masks["um"], masks["allowed_t"],
        masks["ex"], masks["exa"], masks["hs"],
    )


def make_masks(seg_ids, taps, head_count, inner):
    rows = seg_ids.shape[0]
    chunks = rows // LC
    starts = jnp.concatenate(
        [jnp.ones((1,), jnp.int32), (seg_ids[1:] != seg_ids[:-1]).astype(jnp.int32)]
    )
    tri = lax.broadcasted_iota(jnp.int32, (rows, rows), 0) >= lax.broadcasted_iota(
        jnp.int32, (rows, rows), 1
    )
    seq = jnp.sum(jnp.where(tri, starts[None, :], 0), axis=1)
    wide = lambda v: jnp.broadcast_to(v.astype(F32)[:, None], (rows, 128))
    u, um = [], []
    for offset in range(1, taps):
        same = seq[offset:] == seq[:-offset]
        none = jnp.zeros((offset,), jnp.bool_)
        u.append(wide(jnp.concatenate([none, same])))
        um.append(wide(jnp.concatenate([same, none])))
    by_chunk = seq.reshape(chunks, LC)
    order = lax.broadcasted_iota(jnp.int32, (LC, LC), 0)
    other = lax.broadcasted_iota(jnp.int32, (LC, LC), 1)
    same = by_chunk[:, :, None] == by_chunk[:, None, :]
    allowed = (same & (other <= order)[None]).astype(F32).reshape(rows, LC)
    allowed_t = (same & (order <= other)[None]).astype(F32).reshape(rows, LC)
    before = jnp.concatenate([jnp.full((1,), -1, jnp.int32), by_chunk[:-1, -1]])
    carried = (by_chunk == before[:, None]).reshape(rows)
    reach = (by_chunk == by_chunk[:, -1:]).reshape(rows)
    head_of = lambda width, size: (
        lax.broadcasted_iota(jnp.int32, (256, width), 1) // size
    )
    slot = lax.broadcasted_iota(jnp.int32, (256, 1), 0)
    part = jnp.where(
        slot < head_count,
        slot,
        jnp.where(
            slot < 2 * head_count,
            slot - head_count,
            jnp.where((slot >= 128) & (slot < 128 + head_count), slot - 128, -1),
        ),
    )
    ex = (part == head_of(inner, HD)).astype(BF16)
    exa = (part == head_of(head_count * 128, 128)).astype(BF16)
    hs = (
        lax.broadcasted_iota(jnp.int32, (inner, 128), 0) // HD
        == lax.broadcasted_iota(jnp.int32, (inner, 128), 1)
    ).astype(BF16)
    return {
        "u": jnp.stack(u),
        "um": jnp.stack(um),
        "allowed": allowed,
        "allowed_t": allowed_t,
        "edges": jnp.stack([wide(carried), wide(reach)]),
        "ex": ex,
        "exa": exa,
        "hs": hs,
        "live": wide(seg_ids >= 0),
    }


def swap(value):
    return lax.ppermute(value, "core", [(0, 1), (1, 0)])


def all_sum(value, axes):
    for axis, size in axes:
        step = 1
        while step < size:
            value = value + lax.ppermute(value, axis, [(i, i ^ step) for i in range(size)])
            step *= 2
    return value


def local(
    sizes,
    hidden_in,
    seg_ids,
    norm_gain,
    in_weight,
    conv_weight,
    conv_bias,
    dt_bias,
    a_log,
    skip_gain,
    gate_gain,
    out_weight,
    cotangent,
):
    line_n, core_n, shard_n = sizes
    core = lax.axis_index("core")
    rows, width = hidden_in.shape
    inner = gate_gain.shape[0]
    heads = dt_bias.shape[0]
    taps, xbc = conv_weight.shape
    state_dim = (xbc - inner) // 2
    shard_rows = in_weight.shape[0]
    half = shard_rows // 2
    f_rest = in_weight.shape[1] - inner
    f_pad = -f_rest % 128

    def split_cols(value):
        parts = value.reshape(value.shape[0], shard_n, 2, half)
        mine = lax.dynamic_index_in_dim(parts, core, 2, keepdims=False)
        other = lax.dynamic_index_in_dim(parts, 1 - core, 2, keepdims=False)
        flat = (value.shape[0], shard_n * half)
        return mine.reshape(flat), other.reshape(flat)

    def by_core(mine, other):
        first = jnp.where(core == 0, mine, other)
        second = jnp.where(core == 0, other, mine)
        return first, second

    def join_cols(mine, other):
        shape = (mine.shape[0], shard_n, half)
        first, second = by_core(mine.reshape(shape), other.reshape(shape))
        return jnp.stack([first, second], axis=2).reshape(mine.shape[0], width)

    own_rows = lax.dynamic_slice_in_dim(in_weight, core * half, half, 0)
    w1_own = jnp.pad(own_rows[:, inner:], ((0, 0), (0, f_pad)))
    w1_m = lax.all_gather(w1_own, "shard", axis=0, tiled=True)
    w1_o = swap(w1_m)
    w0_m = lax.all_gather(own_rows[:, :inner], "shard", axis=0, tiled=True)
    w0_o = swap(w0_m)
    wo_own, _ = split_cols(out_weight)
    wo_m = lax.all_gather(wo_own, "shard", axis=0, tiled=True)
    wo_o = swap(wo_m)

    masks = make_masks(seg_ids, taps, heads, inner)
    pad_heads = lambda v: jnp.pad(v, (0, 128 - heads))[None]
    dt_bias_p, a_log_p = pad_heads(dt_bias), pad_heads(a_log)
    skip_wide = jnp.repeat(skip_gain, HD)[None]

    hid_m, hid_o = split_cols(hidden_in)
    cot_m, cot_o = split_cols(cotangent)
    gain_m, gain_o = split_cols(norm_gain[None])
    h_m, h_o = hid_m.astype(F32), hid_o.astype(F32)
    square = jnp.sum(h_m * h_m, axis=-1, keepdims=True) + jnp.sum(h_o * h_o, axis=-1, keepdims=True)
    r = lax.rsqrt(square * (1.0 / width) + EPS)
    n_m = (h_m * r * gain_m).astype(BF16)
    n_o = (h_o * r * gain_o).astype(BF16)

    proj1 = (dot(n_m, w1_m) + dot(n_o, w1_o)).astype(BF16)
    saved = run_forward(
        proj1, inner, heads, state_dim, conv_weight, conv_bias[None], dt_bias_p, a_log_p,
        skip_wide, masks,
    )
    gate = (dot(n_m, w0_m) + dot(n_o, w0_o)).astype(BF16)
    d_mixer = (dot(cot_m, wo_m, NT) + dot(cot_o, wo_o, NT)).astype(BF16)
    mixer_out, d_y, d_gate, gg = run_norm(saved[2], gate, d_mixer, gate_gain[None], masks["live"])

    tn = ((0,), (0,))

    def reduce_pair(lhs_m, lhs_o, rhs_m, rhs_o):
        sent = swap(dot(lhs_o, rhs_o, tn).astype(BF16))
        return (dot(lhs_m, rhs_m, tn) + sent.astype(F32)).astype(BF16)

    def reduce_rest(value):
        part = lax.psum_scatter(value, "shard", scatter_dimension=0, tiled=True)
        return lax.psum(part, "line")

    g0 = reduce_rest(reduce_pair(n_m, n_o, d_gate, d_gate))
    go = reduce_rest(reduce_pair(mixer_out, mixer_out, cot_m, cot_o))

    d_x, x_sums, d_bc, bc_sums, d_dt, small = run_backward(
        d_y, saved, proj1, heads, state_dim, conv_weight, dt_bias_p, a_log_p, skip_wide, masks
    )
    d_proj1 = jnp.concatenate([d_x, d_bc, d_dt], axis=1)
    g1 = reduce_rest(reduce_pair(n_m, n_o, d_proj1, d_proj1))

    branch_m, branch_o = dot(mixer_out, wo_m), dot(mixer_out, wo_o)
    block_out = join_cols((h_m + branch_m).astype(BF16), (h_o + branch_o).astype(BF16))

    dn_m = dot(d_gate, w0_m, NT) + dot(d_proj1, w1_m, NT)
    dn_o = dot(d_gate, w0_o, NT) + dot(d_proj1, w1_o, NT)
    ng = join_cols(
        jnp.sum(dn_m * h_m * r, axis=0, keepdims=True), jnp.sum(dn_o * h_o * r, axis=0, keepdims=True)
    )[0]
    gd_m, gd_o = gain_m * dn_m, gain_o * dn_o
    mean = (
        jnp.sum(h_m * gd_m, axis=-1, keepdims=True) + jnp.sum(h_o * gd_o, axis=-1, keepdims=True)
    ) * (1.0 / width)
    back = r * r * r * mean
    input_grad = join_cols(
        cot_m.astype(F32) + r * gd_m - h_m * back, cot_o.astype(F32) + r * gd_o - h_o * back
    )

    sums = jnp.concatenate([x_sums.sum(1), bc_sums.sum(1)], axis=1)
    per_head = small.sum(1)
    packed = jnp.concatenate([sums.reshape(-1), per_head.reshape(-1), gg.sum(0), ng])
    packed = jnp.pad(packed, (0, -packed.shape[0] % 1024)).reshape(-1, 128)
    packed = all_sum(packed, (("core", core_n), ("shard", shard_n), ("line", line_n))).reshape(-1)
    sums = packed[: (taps + 1) * xbc].reshape(taps + 1, xbc)
    at = (taps + 1) * xbc
    per_head = packed[at : at + 384].reshape(3, 128)[:, :heads]
    at += 384
    gate_gain_grad = packed[at : at + inner]
    norm_gain_grad = packed[at + inner : at + inner + width]

    g0_first, g0_second = by_core(g0, swap(g0))
    g1_first, g1_second = by_core(g1[:, :f_rest], swap(g1)[:, :f_rest])
    in_grad = jnp.concatenate(
        [
            jnp.concatenate([g0_first, g1_first], axis=1),
            jnp.concatenate([g0_second, g1_second], axis=1),
        ],
        axis=0,
    ).astype(F32)
    out_grad = join_cols(go, swap(go)).astype(F32)
    return (
        block_out,
        input_grad,
        norm_gain_grad,
        in_grad,
        sums[1:][::-1],
        sums[0],
        per_head[0],
        per_head[1],
        per_head[2],
        gate_gain_grad,
        out_grad,
    )


def solution(mesh):
    rep_n, shard_n = mesh.devices.shape
    sizes = (rep_n // 2, 2, shard_n)
    fine = Mesh(mesh.devices.reshape(sizes), ("line", "core", "shard"))
    tokens = ("line", "core", "shard")
    placed = (
        P(tokens, None),
        P(tokens),
        P(),
        P("shard", None),
        P(),
        P(),
        P(),
        P(),
        P(),
        P(),
        P("shard", None),
        P(tokens, None),
    )
    return jax.shard_map(
        partial(local, sizes),
        mesh=fine,
        in_specs=placed,
        out_specs=(
            P(tokens, None),
            P(tokens, None),
            P(),
            P("shard", None),
            P(),
            P(),
            P(),
            P(),
            P(),
            P(),
            P("shard", None),
        ),
        check_vma=False,
    )
```

```python
from functools import partial

import jax
import jax.numpy as jnp
from jax import lax
from jax.experimental import pallas as pl
from jax.experimental.pallas import tpu as pltpu
from jax.sharding import Mesh, PartitionSpec as P


EPS = 1e-05
HIGHEST = lax.Precision.HIGHEST
F32 = jnp.float32
BF16 = jnp.bfloat16
LC = 128
HEADS_STEP = 8
HD = 64


def dot(a, b, dims=((1,), (0,)), precision=None):
    return lax.dot_general(
        a, b, (dims, ((), ())), preferred_element_type=F32, precision=precision
    )


NT = ((1,), (1,))


def sigmoid(v):
    return 0.5 * jnp.tanh(0.5 * v) + 0.5


def silu_and_slope(pre):
    s = sigmoid(pre)
    value = pre * s
    return value, s + value * (1.0 - s)


def split3(value, head_count):
    lane = lax.broadcasted_iota(jnp.int32, value.shape, 1)
    value = jnp.where(lane < head_count, value, 0.0)
    hi = value.astype(BF16)
    rest = value - hi.astype(F32)
    mid = rest.astype(BF16)
    low = (rest - mid.astype(F32)).astype(BF16)
    first = (hi.astype(F32) + pltpu.roll(mid.astype(F32), head_count, 1)).astype(BF16)
    return jnp.concatenate([first, low], axis=1)


def conv_forward(padded, row, lanes, weight, bias, taps, masks, rows):
    window = padded[pl.ds(row, rows + 8), lanes]
    pre = bias + weight[taps - 1 : taps, :] * window[8 : 8 + rows, :]
    for offset in range(1, taps):
        pre = pre + weight[taps - 1 - offset : taps - offset, :] * (
            window[8 - offset : 8 - offset + rows, :] * masks[offset - 1, pl.ds(row, rows), :]
        )
    return pre


def forward_kernel(
    head_count,
    x_in, bc_in, dt_in, wx, bx, wbc, bbc, dt_bias, a_log, skip, u_ref, allowed, edges, ex, exa,
    x_out, slope_out, y_out, s0_out, bc_out, bcs_out, stack_out, heads_out, at_out,
    padded, cb, bt, xdt, xw, state, d1, ea, ew, ax,
):
    rows = x_in.shape[0]
    chunks = rows // LC
    width = x_in.shape[1]
    taps = wx.shape[0]
    group = pl.program_id(0)

    @pl.when(group == 0)
    def _():
        padded[0:8, :] = jnp.zeros((8, width), F32)
        padded[8:, 0:256] = bc_in[...].astype(F32)
        tri = (
            lax.broadcasted_iota(jnp.int32, (LC, LC), 0)
            >= lax.broadcasted_iota(jnp.int32, (LC, LC), 1)
        ).astype(F32)
        for c in range(chunks):
            row = c * LC
            here = slice(row, row + LC)
            for t in range(2):
                lanes = slice(t * 128, t * 128 + 128)
                pre = conv_forward(
                    padded, row, lanes, wbc[:, lanes], bbc[:, lanes], taps, u_ref, LC
                )
                value, slope = silu_and_slope(pre)
                bc_out[here, lanes] = value.astype(BF16)
                bcs_out[here, lanes] = slope
            writer = bc_out[here, 0:128]
            reader = bc_out[here, 128:256]
            cb[here, :] = dot(reader, writer, NT) * allowed[here, :]
            bt[:, here] = writer.astype(F32).T.astype(BF16)
            v = dt_in[here, :].astype(F32) + dt_bias[...]
            step = jnp.maximum(v, 0.0) + jnp.log1p(jnp.exp(-jnp.abs(v)))
            decay = -jnp.exp(a_log[...]) * step
            a = dot(tri, decay, precision=HIGHEST)
            last = a[LC - 1 : LC, :]
            heads_out[0, here, :] = step
            heads_out[1, here, :] = decay
            at_out[c] = a.T
            stack_out[0, here, :] = split3(step, head_count)
            stack_out[1, here, :] = split3(jnp.exp(a) * edges[0, here, :], head_count)
            stack_out[2, here, :] = split3(jnp.exp(last - a) * edges[1, here, :], head_count)
            stack_out[3, here, :] = split3(a, head_count)

    padded[8:, :] = x_in[...].astype(F32)
    state[...] = jnp.zeros_like(state)

    def chunk(c, carry):
        row = pl.multiple_of(c * LC, LC)
        here = pl.ds(row, LC)
        d1[...] = dot(stack_out[0, here, :], ex[...])
        ea[...] = dot(stack_out[1, here, :], ex[...])
        ew[...] = dot(stack_out[2, here, :], ex[...])
        ax[...] = dot(stack_out[3, here, :], exa[...])
        s0 = state[...].astype(BF16)
        s0_out[pl.ds(c, 1), :, :] = s0[None]
        low = lax.broadcasted_iota(jnp.int32, (LC, 128), 1) < HD
        for p in range(width // 128):
            lanes = slice(p * 128, p * 128 + 128)
            pre = conv_forward(padded, row, lanes, wx[:, lanes], bx[:, lanes], taps, u_ref, LC)
            value, slope = silu_and_slope(pre)
            x_out[here, lanes] = value.astype(BF16)
            slope_out[here, lanes] = slope.astype(BF16)
            scaled = value * d1[:, lanes]
            xdt[:, lanes] = scaled.astype(BF16)
            xw[:, lanes] = (scaled * ew[:, lanes]).astype(BF16)
        reader = bc_out[here, 128:256]
        inter = dot(reader, s0)
        scores = cb[here, :]
        ats = at_out[c, pl.ds(pl.multiple_of(group * HEADS_STEP, 8), HEADS_STEP), :]
        for p in range(width // 128):
            lanes = slice(p * 128, p * 128 + 128)
            mixes = []
            for k in range(2):
                head = 2 * p + k
                arow = ats[head : head + 1, :]
                acol = ax[:, head * 128 : head * 128 + 128]
                mixes.append((jnp.exp(jnp.minimum(acol - arow, 0.0)) * scores).astype(BF16))
            pair = xdt[:, lanes]
            zero = jnp.zeros_like(pair)
            both = jnp.concatenate([jnp.where(low, pair, zero), jnp.where(low, zero, pair)], axis=0)
            y = dot(jnp.concatenate(mixes, axis=1), both)
            y = y + ea[:, lanes] * inter[:, lanes]
            y = y + skip[:, lanes] * x_out[here, lanes].astype(F32)
            y_out[here, lanes] = y.astype(BF16)
        state[...] = state[...] * ea[LC - 1 : LC, :] + dot(bt[:, here], xw[...])
        return carry

    lax.fori_loop(0, chunks, chunk, 0)


def run_forward(proj, inner, head_count, state_dim, conv_w, conv_b, dt_bias, a_log, skip, masks):
    rows = proj.shape[0]
    chunks = rows // LC
    width = HEADS_STEP * HD
    groups = inner // width
    taps = conv_w.shape[0]
    bc = 2 * state_dim
    const = lambda *index: (lambda g: index)
    full = lambda shape: pl.BlockSpec(shape, lambda g: (0,) * len(shape))
    col = lambda lead: pl.BlockSpec((lead, width), lambda g: (0, g))
    out_shape = (
        jax.ShapeDtypeStruct((rows, inner), BF16),
        jax.ShapeDtypeStruct((rows, inner), BF16),
        jax.ShapeDtypeStruct((rows, inner), BF16),
        jax.ShapeDtypeStruct((chunks, state_dim, inner), BF16),
        jax.ShapeDtypeStruct((rows, bc), BF16),
        jax.ShapeDtypeStruct((rows, bc), F32),
        jax.ShapeDtypeStruct((4, rows, 256), BF16),
        jax.ShapeDtypeStruct((2, rows, 128), F32),
        jax.ShapeDtypeStruct((chunks, 128, LC), F32),
    )
    return pl.pallas_call(
        partial(forward_kernel, head_count),
        grid=(groups,),
        in_specs=[
            col(rows),
            pl.BlockSpec((rows, bc), const(0, inner // bc)),
            pl.BlockSpec((rows, 128), const(0, (inner + bc) // 128)),
            col(taps),
            col(1),
            pl.BlockSpec((taps, bc), const(0, inner // bc)),
            pl.BlockSpec((1, bc), const(0, inner // bc)),
            full((1, 128)),
            full((1, 128)),
            col(1),
            full((taps - 1, rows, 128)),
            full((rows, 128)),
            full((2, rows, 128)),
            col(256),
            pl.BlockSpec((256, HEADS_STEP * 128), lambda g: (0, g)),
        ],
        out_specs=[
            col(rows),
            col(rows),
            col(rows),
            pl.BlockSpec((chunks, state_dim, width), lambda g: (0, 0, g)),
            full((rows, bc)),
            full((rows, bc)),
            full((4, rows, 256)),
            full((2, rows, 128)),
            full((chunks, 128, LC)),
        ],
        out_shape=out_shape,
        scratch_shapes=[
            pltpu.VMEM((rows + 8, width), F32),
            pltpu.VMEM((rows, 128), F32),
            pltpu.VMEM((state_dim, rows), BF16),
            pltpu.VMEM((LC, width), BF16),
            pltpu.VMEM((LC, width), BF16),
            pltpu.VMEM((state_dim, width), F32),
            pltpu.VMEM((LC, width), F32),
            pltpu.VMEM((LC, width), F32),
            pltpu.VMEM((LC, width), F32),
            pltpu.VMEM((LC, HEADS_STEP * 128), F32),
        ],
        cost_estimate=pl.CostEstimate(
            flops=20_000_000_000, bytes_accessed=20_000_000, transcendentals=0
        ),
        name="scan_forward",
    )(
        proj, proj, proj, conv_w, conv_b, conv_w, conv_b, dt_bias, a_log, skip,
        masks["u"], masks["allowed"], masks["edges"], masks["ex"], masks["exa"],
    )


def norm_kernel(taps, y_ref, z_ref, dm_ref, gain, live_ref, mixer_out, d_y, d_z, gg_out, gated_s, gg_s):
    rows = y_ref.shape[0]
    inner = y_ref.shape[1]
    tiles = inner // 128
    live = live_ref[...]
    square = jnp.zeros((rows, 128), F32)
    mixed = jnp.zeros((rows, 128), F32)
    for t in range(tiles):
        lanes = slice(t * 128, t * 128 + 128)
        z = z_ref[:, lanes].astype(F32)
        gated = y_ref[:, lanes].astype(F32) * (z * sigmoid(z))
        gated_s[:, lanes] = gated
        square = square + gated * gated
        mixed = mixed + gated * (gain[:, lanes] * (dm_ref[:, lanes].astype(F32) * live))
    q = lax.rsqrt(jnp.sum(square, axis=1, keepdims=True) * (1.0 / inner) + EPS)
    r = jnp.sum(mixed, axis=1, keepdims=True) * (1.0 / inner)
    q = jnp.broadcast_to(q, (rows, 128))
    back = q * q * q * r
    keep = q * live

    @pl.when(pl.program_id(0) == 0)
    def _():
        gg_s[...] = jnp.zeros_like(gg_s)

    for t in range(tiles):
        lanes = slice(t * 128, t * 128 + 128)
        z = z_ref[:, lanes].astype(F32)
        s = sigmoid(z)
        gate = z * s
        slope = s + gate * (1.0 - s)
        gated = gated_s[:, lanes]
        scale = gain[:, lanes]
        mixer_out[:, lanes] = (gated * keep * scale).astype(BF16)
        m = dm_ref[:, lanes].astype(F32) * keep
        gg_s[:, lanes] += jnp.sum((m * gated).reshape(rows // 8, 8, 128), axis=0)
        d_gated = m * scale - gated * back
        d_y[:, lanes] = (d_gated * gate).astype(BF16)
        d_z[:, lanes] = (d_gated * y_ref[:, lanes].astype(F32) * slope).astype(BF16)

    @pl.when(pl.program_id(0) == pl.num_programs(0) - 1)
    def _():
        line = lax.broadcasted_iota(jnp.int32, gg_out.shape, 0)
        gg_out[...] = jnp.where(line == taps + 1, jnp.sum(gg_s[...], axis=0, keepdims=True), 0.0)


def run_norm(y, z, d_mixer, gain, live, taps):
    rows, inner = y.shape
    block = 128
    spec = pl.BlockSpec((block, inner), lambda i: (i, 0))
    return pl.pallas_call(
        partial(norm_kernel, taps),
        grid=(rows // block,),
        in_specs=[
            spec, spec, spec,
            pl.BlockSpec((1, inner), lambda i: (0, 0)),
            pl.BlockSpec((block, 128), lambda i: (i, 0)),
        ],
        out_specs=[spec, spec, spec, pl.BlockSpec((8, inner), lambda i: (0, 0))],
        out_shape=(
            jax.ShapeDtypeStruct((rows, inner), BF16),
            jax.ShapeDtypeStruct((rows, inner), BF16),
            jax.ShapeDtypeStruct((rows, inner), BF16),
            jax.ShapeDtypeStruct((8, inner), F32),
        ),
        scratch_shapes=[pltpu.VMEM((block, inner), F32), pltpu.VMEM((8, inner), F32)],
        cost_estimate=pl.CostEstimate(
            flops=10_000_000_000, bytes_accessed=20_000_000, transcendentals=0
        ),
        name="gated_norm",
    )(y, z, d_mixer, gain, live)


def conv_backward(padded, row, lanes, x_ref, weight, taps, masks):
    x = x_ref[pl.ds(row, LC), lanes].astype(F32)
    window = padded[pl.ds(row, LC + 8), lanes]
    d0 = window[0:LC, :]
    fold = lambda v: jnp.sum(v.reshape(LC // 8, 8, 128), axis=0)
    result = weight[taps - 1 : taps, :] * d0
    sums = [fold(d0 * x)]
    for offset in range(1, taps):
        moved = window[offset : offset + LC, :] * masks[offset - 1, pl.ds(row, LC), :]
        result = result + weight[taps - 1 - offset : taps - offset, :] * moved
        sums.insert(0, fold(moved * x))
    return result, sums + [fold(d0)]


KEPT = 7


def fold_rows(sums, width):
    line = lax.broadcasted_iota(jnp.int32, (8, width), 0)
    result = jnp.zeros((8, width), F32)
    for k in range(sums.shape[0]):
        result = jnp.where(line == k, jnp.sum(sums[k], axis=0, keepdims=True), result)
    return result


def backward_kernel(
    head_count, first_group, opens, closes,
    dy_ref, x_ref, slope_ref, x_in, bc_in, s0_ref, bc_ref, bcs_ref, stack, heads, at_ref, dt_in,
    wx, wbc, dt_bias, a_log, skip, um_ref, allowed_t, ex, exa, hs,
    *rest,
):
    kept_in, rest = ((), rest) if opens else (rest[:KEPT], rest[KEPT:])
    dx_out, sums_out, rest = rest[0], rest[1], rest[2:]
    if closes:
        (dbc_out, sums_bc_out, ddt_out, small_out), rest = rest[:4], rest[4:]
        kept, rest = rest[:KEPT], rest[KEPT:]
    else:
        kept, rest = rest[:KEPT], rest[KEPT:]
    dcbt, d_writer, d_reader, prow, qcol, hsum, sgrow = kept
    (
        padded, sums_s, grad, cbt, ct, d1, ea, ew, ax, inter, gb, dye, xdt, xw, sacc,
    ) = rest
    rows = x_ref.shape[0]
    chunks = rows // LC
    width = x_ref.shape[1]
    taps = wx.shape[0]
    group = pl.program_id(0) + first_group
    tiles = width // 128

    @pl.when(pl.program_id(0) == 0)
    def _():
        padded[rows:, :] = jnp.zeros((8, width), F32)
        for c in range(chunks):
            here = slice(c * LC, c * LC + LC)
            writer = bc_ref[here, 0:128]
            reader = bc_ref[here, 128:256]
            cbt[here, :] = dot(writer, reader, NT) * allowed_t[here, :]
            ct[:, here] = reader.astype(F32).T.astype(BF16)
        for index, ref in enumerate(kept):
            ref[...] = jnp.zeros_like(ref) if opens else kept_in[index][...]

    grad[...] = jnp.zeros_like(grad)
    low = lax.broadcasted_iota(jnp.int32, (LC, 128), 1) < HD
    lane = lax.broadcasted_iota(jnp.int32, (LC, 128), 1)

    def chunk(i, carry):
        c = chunks - 1 - i
        row = pl.multiple_of(c * LC, LC)
        here = pl.ds(row, LC)
        d1[...] = dot(stack[0, here, :], ex[...])
        ea[...] = dot(stack[1, here, :], ex[...])
        ew[...] = dot(stack[2, here, :], ex[...])
        ax[...] = dot(stack[3, here, :], exa[...])
        writer = bc_ref[here, 0:128]
        reader = bc_ref[here, 128:256]
        s0 = s0_ref[c]
        g = grad[...]
        g_low = g.astype(BF16)
        inter[...] = dot(reader, s0)
        gb[...] = dot(writer, g_low) * ew[...]
        fold = jnp.sum((s0.astype(F32) * g).reshape(s0.shape[0] // 8, 8, width), axis=0)
        fold = fold * ea[LC - 1 : LC, :]
        sgrow[pl.ds(pl.multiple_of(c * 8, 8), 8), :] += dot(fold.astype(BF16), hs[...])
        for p in range(tiles):
            lanes = slice(p * 128, p * 128 + 128)
            x = x_ref[here, lanes].astype(F32)
            dy = dy_ref[here, lanes].astype(F32)
            scaled = x * d1[:, lanes]
            xdt[:, lanes] = scaled.astype(BF16)
            xw[:, lanes] = (scaled * ew[:, lanes]).astype(BF16)
            weighted = dy * ea[:, lanes]
            dye[:, lanes] = weighted.astype(BF16)
            sacc[1, :, lanes] = (x * gb[:, lanes]).astype(BF16)
            sacc[2, :, lanes] = (weighted * inter[:, lanes]).astype(BF16)
            sacc[3, :, lanes] = (dy * x).astype(BF16)
        d_reader[here, :] += dot(dye[...], s0, NT)
        d_writer[here, :] += dot(xw[...], g_low, NT)
        scores = cbt[here, :]
        group_rows = pl.ds(pl.multiple_of(group * HEADS_STEP, 8), HEADS_STEP)
        ats = at_ref[c, group_rows, :]
        for p in range(tiles):
            lanes = slice(p * 128, p * 128 + 128)
            pair = dy_ref[here, lanes]
            src = xdt[:, lanes]
            zero = jnp.zeros_like(pair)
            src2 = jnp.concatenate([jnp.where(low, src, zero), jnp.where(low, zero, src)], axis=0)
            pair2 = jnp.concatenate([jnp.where(low, pair, zero), jnp.where(low, zero, pair)], axis=0)
            dm = dot(src2, pair, NT)
            mixes = []
            for k in range(2):
                head = 2 * p + k
                index = group * HEADS_STEP + head
                arow = ats[head : head + 1, :]
                acol = ax[:, head * 128 : head * 128 + 128]
                e = jnp.exp(jnp.minimum(arow - acol, 0.0))
                mixes.append((e * scores).astype(BF16))
                t = e * dm[k * LC : k * LC + LC, :]
                dcbt[here, :] += t
                qq = t * scores
                prow.at[c, group_rows, :][head : head + 1, :] = jnp.sum(qq, axis=0, keepdims=True)
                qcol[here, :] = jnp.where(
                    lane == index, jnp.sum(qq, axis=1, keepdims=True), qcol[here, :]
                )
            x = x_ref[here, lanes].astype(F32)
            dxdt = dot(jnp.concatenate(mixes, axis=1), pair2) + gb[:, lanes]
            sacc[0, :, lanes] = (x * dxdt).astype(BF16)
            dx = d1[:, lanes] * dxdt + skip[:, lanes] * pair.astype(F32)
            padded[here, lanes] = dx * slope_ref[here, lanes].astype(F32)
        for k in range(4):
            hsum[k, here, :] += dot(sacc[k], hs[...])
        grad[...] = g * ea[LC - 1 : LC, :] + dot(ct[:, here], dye[...])
        return carry

    lax.fori_loop(0, chunks, chunk, 0)

    sums_s[...] = jnp.zeros_like(sums_s)

    def conv_chunk(c, carry):
        row = pl.multiple_of(c * LC, LC)
        for p in range(tiles):
            lanes = slice(p * 128, p * 128 + 128)
            result, sums = conv_backward(padded, row, lanes, x_in, wx[:, lanes], taps, um_ref)
            dx_out[pl.ds(row, LC), lanes] = result.astype(BF16)
            for k in range(taps + 1):
                sums_s[k, :, lanes] += sums[k]
        return carry

    lax.fori_loop(0, chunks, conv_chunk, 0)
    sums_out[...] = fold_rows(sums_s[...], width)
    if not closes:
        return

    @pl.when(pl.program_id(0) == pl.num_programs(0) - 1)
    def _():
        total_a = jnp.zeros((8, 128), F32)
        total_dt = jnp.zeros((8, 128), F32)
        total_skip = jnp.zeros((8, 128), F32)
        upper = (
            lax.broadcasted_iota(jnp.int32, (LC, LC), 0)
            <= lax.broadcasted_iota(jnp.int32, (LC, LC), 1)
        ).astype(F32)
        at_end = lax.broadcasted_iota(jnp.int32, (LC, 128), 0) == LC - 1
        fold = lambda v: jnp.sum(v.reshape(LC // 8, 8, 128), axis=0)
        sums_s[...] = jnp.zeros_like(sums_s)
        for c in range(chunks):
            here = slice(c * LC, c * LC + LC)
            writer = bc_ref[here, 0:128]
            reader = bc_ref[here, 128:256]
            d_scores = dcbt[here, :] * allowed_t[here, :]
            d_w = d_writer[here, :] + dot(d_scores.astype(BF16), reader)
            d_r = d_reader[here, :] + dot(d_scores.T.astype(BF16), writer)
            padded[here, 0:128] = d_w * bcs_ref[here, 0:128]
            padded[here, 128:256] = d_r * bcs_ref[here, 128:256]
            step = heads[0, here, :]
            decay = heads[1, here, :]
            q_state = step * hsum[1, here, :]
            da = prow[c].T - qcol[here, :] + hsum[2, here, :] - q_state
            ends = jnp.sum(q_state, axis=0, keepdims=True) + jnp.sum(
                sgrow[c * 8 : c * 8 + 8, :], axis=0, keepdims=True
            )
            da = da + jnp.where(at_end, ends, 0.0)
            d_decay = dot(upper, da, precision=HIGHEST)
            d_step = hsum[0, here, :] - jnp.exp(a_log[...]) * d_decay
            d_raw = d_step * sigmoid(dt_in[here, :].astype(F32) + dt_bias[...])
            d_raw = jnp.where(lane < head_count, d_raw, 0.0)
            ddt_out[here, :] = d_raw.astype(BF16)
            total_dt = total_dt + fold(d_raw)
            total_a = total_a + fold(d_decay * decay)
            total_skip = total_skip + fold(hsum[3, here, :])
        line = lax.broadcasted_iota(jnp.int32, (8, 128), 0)
        result = jnp.zeros((8, 128), F32)
        for k, total in enumerate((total_dt, total_a, total_skip)):
            result = jnp.where(line == k, jnp.sum(total, axis=0, keepdims=True), result)
        small_out[...] = result
        for c in range(chunks):
            row = c * LC
            for p in range(2):
                lanes = slice(p * 128, p * 128 + 128)
                result, sums = conv_backward(padded, row, lanes, bc_in, wbc[:, lanes], taps, um_ref)
                dbc_out[row : row + LC, lanes] = result.astype(BF16)
                for k in range(taps + 1):
                    sums_s[k, :, lanes] += sums[k]
        sums_bc_out[...] = fold_rows(sums_s[:, :, 0:256], 256)


def run_backward(
    dy, saved, proj, head_count, state_dim, conv_w, dt_bias, a_log, skip, masks, span, kept=None
):
    x, slope, _, s0, bc_val, bc_slope, stack, heads, at = saved
    rows, inner = dy.shape
    chunks = rows // LC
    width = HEADS_STEP * HD
    first, last = span
    opens, closes = first == 0, last == inner // width
    taps = conv_w.shape[0]
    bc = 2 * state_dim
    const = lambda *index: (lambda g: index)
    full = lambda shape: pl.BlockSpec(shape, lambda g: (0,) * len(shape))
    col = lambda lead: pl.BlockSpec((lead, width), lambda g: (0, g + first))
    own = lambda lead: pl.BlockSpec((lead, width), lambda g: (0, g))
    kept_shapes = [
        (rows, 128), (rows, 128), (rows, 128), (chunks, 128, LC), (rows, 128), (4, rows, 128),
        (chunks * 8, 128),
    ]
    out_specs = [own(rows), own(8)]
    out_shape = [
        jax.ShapeDtypeStruct((rows, (last - first) * width), BF16),
        jax.ShapeDtypeStruct((8, (last - first) * width), F32),
    ]
    scratch = [
        pltpu.VMEM((rows + 8, width), F32),
        pltpu.VMEM((taps + 1, 8, width), F32),
        pltpu.VMEM((state_dim, width), F32),
        pltpu.VMEM((rows, 128), F32),
        pltpu.VMEM((state_dim, rows), BF16),
        pltpu.VMEM((LC, width), F32),
        pltpu.VMEM((LC, width), F32),
        pltpu.VMEM((LC, width), F32),
        pltpu.VMEM((LC, HEADS_STEP * 128), F32),
        pltpu.VMEM((LC, width), F32),
        pltpu.VMEM((LC, width), F32),
        pltpu.VMEM((LC, width), BF16),
        pltpu.VMEM((LC, width), BF16),
        pltpu.VMEM((LC, width), BF16),
        pltpu.VMEM((4, LC, width), BF16),
    ]
    if closes:
        shapes = [((rows, bc), BF16), ((8, bc), F32), ((rows, 128), BF16), ((8, 128), F32)]
        scratch = [pltpu.VMEM(shape, F32) for shape in kept_shapes] + scratch
    else:
        shapes = [(shape, F32) for shape in kept_shapes]
    out_specs += [full(shape) for shape, _ in shapes]
    out_shape += [jax.ShapeDtypeStruct(shape, kind) for shape, kind in shapes]
    share = (last - first) * width / inner
    return pl.pallas_call(
        partial(backward_kernel, head_count, first, opens, closes),
        grid=(last - first,),
        in_specs=[
            col(rows),
            col(rows),
            col(rows),
            col(rows),
            pl.BlockSpec((rows, bc), const(0, inner // bc)),
            pl.BlockSpec((chunks, state_dim, width), lambda g: (0, 0, g + first)),
            full((rows, bc)),
            full((rows, bc)),
            full((4, rows, 256)),
            full((2, rows, 128)),
            full((chunks, 128, LC)),
            pl.BlockSpec((rows, 128), const(0, (inner + bc) // 128)),
            col(taps),
            pl.BlockSpec((taps, bc), const(0, inner // bc)),
            full((1, 128)),
            full((1, 128)),
            col(1),
            full((taps - 1, rows, 128)),
            full((rows, 128)),
            col(256),
            pl.BlockSpec((256, HEADS_STEP * 128), lambda g: (0, g + first)),
            pl.BlockSpec((width, 128), lambda g: (g + first, 0)),
        ]
        + ([] if opens else [full(shape) for shape in kept_shapes]),
        out_specs=out_specs,
        out_shape=out_shape,
        scratch_shapes=scratch,
        cost_estimate=pl.CostEstimate(
            flops=int(40e9 * share), bytes_accessed=int(20e6 * share), transcendentals=0
        ),
        name="scan_backward",
    )(
        dy, x, slope, proj, proj, s0, bc_val, bc_slope, stack, heads, at, proj,
        conv_w, conv_w, dt_bias, a_log, skip, masks["um"], masks["allowed_t"],
        masks["ex"], masks["exa"], masks["hs"], *(() if opens else kept),
    )


def join_kernel(axis, core_ref, *refs):
    out = refs[-1]
    own = (pl.program_id(0) // axis == core_ref[0]).astype(F32)
    at = 0
    for mine, other in zip(refs[0:-1:2], refs[1:-1:2]):
        width = min(mine.shape[1], out.shape[1] - at)
        value = jnp.where(own > 0.5, mine[:, 0:width].astype(F32), other[:, 0:width].astype(F32))
        out[:, at : at + width] = value
        at += width


def join_rows(core, pairs, width):
    rows = pairs[0][0].shape[0]
    block = 48
    steps = rows // block
    specs, args = [], []
    for pair in pairs:
        for value in pair:
            specs.append(pl.BlockSpec((block, value.shape[1]), lambda i, c: (i % steps, 0)))
            args.append(value)
    return pl.pallas_call(
        partial(join_kernel, steps),
        grid_spec=pltpu.PrefetchScalarGridSpec(
            num_scalar_prefetch=1,
            grid=(2 * steps,),
            in_specs=specs,
            out_specs=pl.BlockSpec((block, width), lambda i, c: (i, 0)),
        ),
        out_shape=jax.ShapeDtypeStruct((2 * rows, width), F32),
        cost_estimate=pl.CostEstimate(
            flops=1_000_000, bytes_accessed=20_000_000, transcendentals=0
        ),
        name="join_rows",
    )(core.reshape(1), *args)


def join_cols_kernel(core_ref, mine, other, out):
    half = mine.shape[1]
    first = core_ref[0] == 0
    a, b = mine[...].astype(F32), other[...].astype(F32)
    out[:, 0:half] = jnp.where(first, a, b)
    out[:, half:] = jnp.where(first, b, a)


def join_cols(core, mine, other):
    rows, half = mine.shape
    block = 128
    spec = pl.BlockSpec((block, half), lambda i, c: (i, 0))
    return pl.pallas_call(
        join_cols_kernel,
        grid_spec=pltpu.PrefetchScalarGridSpec(
            num_scalar_prefetch=1,
            grid=(rows // block,),
            in_specs=[spec, spec],
            out_specs=pl.BlockSpec((block, 2 * half), lambda i, c: (i, 0)),
        ),
        out_shape=jax.ShapeDtypeStruct((rows, 2 * half), F32),
        cost_estimate=pl.CostEstimate(
            flops=1_000_000, bytes_accessed=8_000_000, transcendentals=0
        ),
        name="join_cols",
    )(core.reshape(1), mine, other)


def make_masks(seg_ids, taps, head_count, inner):
    rows = seg_ids.shape[0]
    chunks = rows // LC
    starts = jnp.concatenate(
        [jnp.ones((1,), jnp.int32), (seg_ids[1:] != seg_ids[:-1]).astype(jnp.int32)]
    )
    tri = lax.broadcasted_iota(jnp.int32, (rows, rows), 0) >= lax.broadcasted_iota(
        jnp.int32, (rows, rows), 1
    )
    seq = jnp.sum(jnp.where(tri, starts[None, :], 0), axis=1)
    wide = lambda v: jnp.broadcast_to(v.astype(F32)[:, None], (rows, 128))
    u, um = [], []
    for offset in range(1, taps):
        same = seq[offset:] == seq[:-offset]
        none = jnp.zeros((offset,), jnp.bool_)
        u.append(wide(jnp.concatenate([none, same])))
        um.append(wide(jnp.concatenate([same, none])))
    by_chunk = seq.reshape(chunks, LC)
    order = lax.broadcasted_iota(jnp.int32, (LC, LC), 0)
    other = lax.broadcasted_iota(jnp.int32, (LC, LC), 1)
    same = by_chunk[:, :, None] == by_chunk[:, None, :]
    allowed = (same & (other <= order)[None]).astype(F32).reshape(rows, LC)
    allowed_t = (same & (order <= other)[None]).astype(F32).reshape(rows, LC)
    before = jnp.concatenate([jnp.full((1,), -1, jnp.int32), by_chunk[:-1, -1]])
    carried = (by_chunk == before[:, None]).reshape(rows)
    reach = (by_chunk == by_chunk[:, -1:]).reshape(rows)
    head_of = lambda width, size: (
        lax.broadcasted_iota(jnp.int32, (256, width), 1) // size
    )
    slot = lax.broadcasted_iota(jnp.int32, (256, 1), 0)
    part = jnp.where(
        slot < head_count,
        slot,
        jnp.where(
            slot < 2 * head_count,
            slot - head_count,
            jnp.where((slot >= 128) & (slot < 128 + head_count), slot - 128, -1),
        ),
    )
    ex = (part == head_of(inner, HD)).astype(BF16)
    exa = (part == head_of(head_count * 128, 128)).astype(BF16)
    hs = (
        lax.broadcasted_iota(jnp.int32, (inner, 128), 0) // HD
        == lax.broadcasted_iota(jnp.int32, (inner, 128), 1)
    ).astype(BF16)
    return {
        "u": jnp.stack(u),
        "um": jnp.stack(um),
        "allowed": allowed,
        "allowed_t": allowed_t,
        "edges": jnp.stack([wide(carried), wide(reach)]),
        "ex": ex,
        "exa": exa,
        "hs": hs,
        "live": wide(seg_ids >= 0),
    }


TN = ((0,), (0,))


def swap(value):
    return lax.ppermute(value, "core", [(0, 1), (1, 0)])


def to_partner(value, axis, size, step):
    return lax.ppermute(value, axis, [(i, i ^ step) for i in range(size)])


def after(value, *others):
    return lax.optimization_barrier((value,) + others)[0]


def line_sum(value, size):
    step = 1
    while step < size:
        moved = to_partner(value, "line", size, step)
        value = (value.astype(F32) + moved.astype(F32)).astype(value.dtype)
        step *= 2
    return value


def pick(value, index, axis=0):
    return lax.dynamic_index_in_dim(value, index, axis, keepdims=False)


def local(
    sizes,
    hidden_in,
    seg_ids,
    norm_gain,
    in_weight,
    conv_weight,
    conv_bias,
    dt_bias,
    a_log,
    skip_gain,
    gate_gain,
    out_weight,
    cotangent,
):
    line_n, core_n, shard_n = sizes
    core = lax.axis_index("core")
    shard = lax.axis_index("shard")
    _, width = hidden_in.shape
    inner = gate_gain.shape[0]
    heads = dt_bias.shape[0]
    taps, xbc = conv_weight.shape
    state_dim = (xbc - inner) // 2
    half = in_weight.shape[0] // 2
    quarter = half // 2
    out_half = width // 2
    f_rest = in_weight.shape[1] - inner
    f_pad = -f_rest % 128
    f_wide = f_rest + f_pad

    def split_rows(value):
        parts = value.reshape(value.shape[0], shard_n, 2, half)
        flat = (value.shape[0], shard_n * half)
        return pick(parts, core, 2).reshape(flat), pick(parts, 1 - core, 2).reshape(flat)

    def join_split(mine, other):
        shape = (mine.shape[0], shard_n, half)
        mine, other = mine.reshape(shape), other.reshape(shape)
        first = jnp.where(core == 0, mine, other)
        second = jnp.where(core == 0, other, mine)
        return jnp.stack([first, second], axis=2).reshape(mine.shape[0], width)

    def halves(value):
        parts = value.reshape(value.shape[0], 2, out_half)
        return pick(parts, core, 1), pick(parts, 1 - core, 1)

    own = jnp.pad(in_weight[:, inner:], ((0, 0), (0, f_pad)))
    piece = pick(own.reshape(2, half, f_wide), core)
    from_x = to_partner(piece, "shard", shard_n, 1)
    from_y = to_partner(piece, "shard", shard_n, 2)
    far_a = to_partner(from_y[:quarter], "shard", shard_n, 1)
    far_b = to_partner(from_x[quarter:], "shard", shard_n, 2)
    w1 = jnp.zeros((4 * shard_n, quarter, f_wide), BF16)

    def put(whole, value, owner, which, part=0):
        value = value.reshape(-1, quarter, f_wide)
        return lax.dynamic_update_slice_in_dim(whole, value, owner * 4 + which * 2 + part, 0)

    w1 = put(w1, own, shard, 0)
    w1 = put(w1, from_x, shard ^ 1, core)
    w1 = put(w1, from_y, shard ^ 2, core)
    w1 = put(w1, swap(from_x), shard ^ 1, 1 - core)
    w1 = put(w1, swap(from_y), shard ^ 2, 1 - core)
    w1 = put(w1, far_a, shard ^ 3, core)
    w1 = put(w1, far_b, shard ^ 3, core, 1)
    w1 = put(w1, swap(far_a), shard ^ 3, 1 - core)
    w1 = put(w1, swap(far_b), shard ^ 3, 1 - core, 1)
    w1 = w1.reshape(width, f_wide)

    own0 = pick(in_weight.reshape(2, half, -1)[:, :, :inner], core)
    w0_m = lax.all_gather(own0, "shard", axis=0, tiled=True)
    w0_o = swap(w0_m)
    own_out, _ = halves(out_weight)
    wo_m = lax.all_gather(own_out, "shard", axis=0, tiled=True)
    wo_o = swap(wo_m)

    masks = make_masks(seg_ids, taps, heads, inner)
    pad_heads = lambda v: jnp.pad(v, (0, 128 - heads))[None]
    dt_bias_p, a_log_p = pad_heads(dt_bias), pad_heads(a_log)
    skip_wide = jnp.repeat(skip_gain, HD)[None]

    cot_m, cot_o = halves(cotangent)
    hidden = hidden_in.astype(F32)
    r = lax.rsqrt(jnp.mean(hidden * hidden, axis=-1, keepdims=True) + EPS)
    normed = (hidden * r * norm_gain).astype(BF16)
    n_m, n_o = split_rows(normed)

    proj1 = dot(normed, w1).astype(BF16)
    saved = run_forward(
        proj1, inner, heads, state_dim, conv_weight, conv_bias[None], dt_bias_p, a_log_p,
        skip_wide, masks,
    )
    n_m2, n_o2 = lax.optimization_barrier((n_m, n_o, saved[2]))[:2]
    gate = (dot(n_m2, w0_m) + dot(n_o2, w0_o)).astype(BF16)
    cot_m2, cot_o2 = lax.optimization_barrier((cot_m, cot_o, gate))[:2]
    d_mixer = (dot(cot_m2, wo_m, NT) + dot(cot_o2, wo_o, NT)).astype(BF16)
    mixer_out, d_y, d_gate, gg = run_norm(
        saved[2], gate, d_mixer, gate_gain[None], masks["live"], taps
    )

    def reduce_pair(lhs_m, lhs_o, rhs_m, rhs_o):
        sent = swap(dot(lhs_o, rhs_o, TN).astype(BF16))
        return (dot(lhs_m, rhs_m, TN) + sent.astype(F32)).astype(BF16)

    def scatter(value):
        return lax.psum_scatter(value, "shard", scatter_dimension=0, tiled=True)

    go_pair = reduce_pair(mixer_out, mixer_out, cot_m, cot_o)
    go = scatter(go_pair)
    g0_pair = reduce_pair(n_m, n_o, after(d_gate, go_pair), d_gate)
    g0 = scatter(g0_pair)

    groups = inner // (HEADS_STEP * HD)
    cut = (2 * groups) // 3
    first = run_backward(
        after(d_y, g0_pair), saved, proj1, heads, state_dim, conv_weight, dt_bias_p, a_log_p,
        skip_wide, masks, (0, cut),
    )
    d_xa, sums_a, kept = first[0], first[1], first[2:]
    ga_pair = reduce_pair(n_m, n_o, d_xa, d_xa)
    ga = scatter(ga_pair)
    d_xb, sums_b, d_bc, sums_bc, d_dt, small = run_backward(
        d_y, saved, proj1, heads, state_dim, conv_weight, dt_bias_p, a_log_p, skip_wide,
        masks, (cut, groups), kept,
    )
    d_last = jnp.concatenate([d_xb, d_bc, d_dt], axis=1)
    gb_pair = reduce_pair(n_m, n_o, d_last, d_last)

    ypos, xpos = shard // 2, shard % 2
    blocks = gb_pair.reshape(2, 2, half, -1)
    add = lambda a, b: (a.astype(F32) + b.astype(F32)).astype(BF16)
    upper, lower = blocks[:, :, :quarter], blocks[:, :, quarter:]
    up = add(pick(upper, xpos, 1), to_partner(pick(upper, 1 - xpos, 1), "shard", shard_n, 1))
    lo = add(pick(lower, ypos, 0), to_partner(pick(lower, 1 - ypos, 0), "shard", shard_n, 2))
    up = add(pick(up, ypos), to_partner(pick(up, 1 - ypos), "shard", shard_n, 2))
    lo = add(pick(lo, xpos), to_partner(pick(lo, 1 - xpos), "shard", shard_n, 1))
    gb = line_sum(jnp.concatenate([up, lo], axis=0), line_n)
    go, g0, ga = line_sum(go, line_n), line_sum(g0, line_n), line_sum(ga, line_n)

    branch_m, branch_o = dot(mixer_out, wo_m), dot(mixer_out, wo_o)
    block_out = (hidden + join_cols(core, branch_m, branch_o)).astype(BF16)

    d_proj1 = jnp.concatenate([d_xa, d_last], axis=1)
    dn = dot(d_proj1, w1, NT) + join_split(dot(d_gate, w0_m, NT), dot(d_gate, w0_o, NT))
    ng = jnp.sum(dn * (hidden * r), axis=0, keepdims=True)
    gd = norm_gain * dn
    mean = jnp.mean(hidden * gd, axis=-1, keepdims=True)
    input_grad = cotangent.astype(F32) + r * gd - hidden * (r * r * r * mean)

    packed = jnp.concatenate(
        [jnp.concatenate([sums_a, sums_b], axis=1) + gg, sums_bc], axis=1
    )
    tail = jnp.concatenate([ng, small[0:1], small[1:2], small[2:3]], axis=1)
    tail = jnp.pad(tail, ((taps + 2, 8 - taps - 3), (0, xbc - tail.shape[1])))
    packed = packed + tail
    for axis, size in (("core", core_n), ("shard", shard_n), ("line", line_n)):
        packed = line_sum_on(packed, axis, size)
    last = packed[taps + 2]

    outs = (
        block_out,
        input_grad,
        last[:width],
        packed[:taps],
        packed[taps],
        last[width : width + heads],
        last[width + 128 : width + 128 + heads],
        last[width + 256 : width + 256 + heads],
        packed[taps + 1, :inner],
        join_cols(core, go, swap(go)),
    )
    pairs = [(g0, swap(g0)), (ga, swap(ga)), (gb, swap(gb))]
    in_grad = join_rows(core, pairs, inner + f_rest)
    return outs[:3] + (in_grad,) + outs[3:]


def line_sum_on(value, axis, size):
    step = 1
    while step < size:
        value = value + to_partner(value, axis, size, step)
        step *= 2
    return value


def solution(mesh):
    rep_n, shard_n = mesh.devices.shape
    sizes = (rep_n // 2, 2, shard_n)
    fine = Mesh(mesh.devices.reshape(sizes), ("line", "core", "shard"))
    tokens = ("line", "core", "shard")
    placed = (
        P(tokens, None),
        P(tokens),
        P(),
        P("shard", None),
        P(),
        P(),
        P(),
        P(),
        P(),
        P(),
        P("shard", None),
        P(tokens, None),
    )
    return jax.shard_map(
        partial(local, sizes),
        mesh=fine,
        in_specs=placed,
        out_specs=(
            P(tokens, None),
            P(tokens, None),
            P(),
            P("shard", None),
            P(),
            P(),
            P(),
            P(),
            P(),
            P(),
            P("shard", None),
        ),
        check_vma=False,
    )
```
